32 devices in a mesh: seq: 16 (over z, y, x), head: 2 (over core).
Axes of the slice: x: 2, y: 2, z: 4, core: 2. Of those that a mesh axis runs over, the one named last changes fastest.
Arguments:
- queries: bfloat16 [128, 1024], P(None, 'head'), may hold values from -400 to 400
- keys: bfloat16 [4096, 256], P('seq', 'head'), may hold values from -6 to 6
- values: bfloat16 [4096, 256], P('seq', 'head'), may hold values from -6 to 6
- householder: bfloat16 [4096, 256], P('seq', 'head'), may hold values from -6 to 6
- out_proj: bfloat16 [1024, 1024], P('head', 'seq'), may hold values from -0.1875 to 0.1875
Outputs:
- mixed: bfloat16 [128, 1024], P('head', 'seq')
The draws below stay inside these ranges and needn't reach their ends.
All inputs are finite; a program needn't handle non-finite values.
Results may differ from the reference program's by a relative error of at most 0.02.
Values may be sent and summed in bfloat16 or wider, within the bound.
No kernel may reach another device: no remote copies, remote signals or barrier semaphores. Data moves between devices by JAX's collectives and lax.ppermute only.
A program may use at most 64 MiB of HBM per device.

```python
import jax
import jax.numpy as jnp
from jax import lax

HEAD = 128
GROUP = 4
BLOCK = 64
QUERIES = 128
KV = 2
D = 1024
CTX = 4096


def draw_queries(key, part):
    normal_vals = jnp.clip(jax.random.normal(key, (QUERIES, D), jnp.float32), -6.0, 6.0)
    return normal_vals.astype(jnp.bfloat16)


def block_levels(stream_key, extent, shards, smallest, top_value):
    def one(position, blocks):
        steps = jax.random.uniform(jax.random.fold_in(jax.random.fold_in(stream_key, 6), position), (blocks,), jnp.float32, smallest / len(shards), top_value / len(shards))
        return jnp.repeat(jnp.exp(steps), extent[position] // blocks).reshape((-1,) + (1,) * (len(extent) - position - 1))

    level = one(*shards[0])
    for cut in shards[1:]:
        level = level * one(*cut)
    return level


def normal_values(rng, shape, deviation, limit, cuts=(), kind=jnp.bfloat16):
    factor_of = block_levels(rng, shape, cuts, -0.22, 0.18) if cuts else 1.0
    entries = jax.random.normal(rng, shape, jnp.float32) * deviation * factor_of
    return jnp.minimum(jnp.maximum(entries, -limit), limit).astype(kind)


def setup_inputs(seed: int = 0) -> dict:
    seeds = jax.random.split(jax.random.key(seed), 6)
    queries = draw_queries(jax.random.fold_in(seeds[5], 71), 0)
    keys = normal_values(seeds[1], (CTX, KV * HEAD), 1.0, 6.0, ((0, 16), (1, 2)))
    values = normal_values(seeds[2], (CTX, KV * HEAD), 1.0, 6.0, ((0, 16), (1, 2)))
    householder = normal_values(seeds[3], (CTX, KV * HEAD), 1.0, 6.0, ((0, 16), (1, 2)))
    out_proj = normal_values(seeds[4], (D, D), D ** -0.5, 0.1875, ((0, 2), (1, 16)))
    return {"queries": queries, "keys": keys, "values": values, "householder": householder, "out_proj": out_proj}


def unit_rows(raw_vecs):
    return raw_vecs * lax.rsqrt(lax.optimization_barrier(jnp.sum(raw_vecs * raw_vecs, axis=-1, keepdims=True)) + 1e-06)

def span_forms(raw_vecs, keys_float):
    precise = lax.Precision.HIGHEST
    vectors = unit_rows(raw_vecs)
    block_len = vectors.shape[1]
    head_width = vectors.shape[2]
    row_ids = lax.broadcasted_iota(jnp.int32, (block_len, block_len), 0)
    col_ids = lax.broadcasted_iota(jnp.int32, (block_len, block_len), 1)
    gram = jnp.einsum('nad,nbd->nab', vectors, vectors, precision=precise)
    lower = jnp.where(row_ids > col_ids, gram, 0.0) + jnp.where(row_ids == col_ids, 0.5, 0.0)
    identity_block = jnp.broadcast_to(jnp.eye(block_len, dtype=jnp.float32), lower.shape)
    coeff = jax.scipy.linalg.solve_triangular(lower, identity_block, lower=True)
    identity_head = jnp.eye(head_width, dtype=jnp.float32)
    transition = identity_head - jnp.einsum('nad,nab,nbe->nde', vectors, coeff, vectors, precision=precise)
    inner = jnp.einsum('nbd,njd->nbj', vectors, keys_float, precision=precise)
    inner = jnp.where(row_ids > col_ids, inner, 0.0)
    mixing = jnp.einsum('nab,nbj->naj', coeff, inner, precision=precise)
    carried = keys_float - jnp.einsum('naj,nad->njd', mixing, vectors, precision=precise)
    return (transition, carried)

def carry_back(transition, carried, identity_head):
    precise = lax.Precision.HIGHEST

    def advance(running, span_item):
        factor, block_keys = span_item
        emitted = jnp.dot(block_keys, running.T, precision=precise)
        return (jnp.dot(running, factor, precision=precise), emitted)
    return lax.scan(advance, identity_head, (transition, carried), reverse=True)

def reference(queries, keys, values, householder, out_proj):
    precise = lax.Precision.HIGHEST
    columns = []
    blocks = CTX // BLOCK
    identity_head = jnp.eye(HEAD, dtype=jnp.float32)
    for kv_head in range(KV):
        lo_col = kv_head * HEAD
        raw_vecs = householder[:, lo_col:lo_col + HEAD].astype(jnp.float32).reshape(blocks, BLOCK, HEAD)
        keys_float = keys[:, lo_col:lo_col + HEAD].astype(jnp.float32).reshape(blocks, BLOCK, HEAD)
        transition, carried = span_forms(raw_vecs, keys_float)
        _, moved = carry_back(transition, carried, identity_head)
        moved = moved.reshape(CTX, HEAD)
        head_values = values[:, lo_col:lo_col + HEAD]
        for member in range(GROUP):
            q_col = (kv_head * GROUP + member) * HEAD
            query_rows = queries[:, q_col:q_col + HEAD].astype(jnp.float32)
            scores = jnp.dot(query_rows, moved.T, precision=precise) / jnp.sqrt(jnp.float32(HEAD))
            peak = lax.optimization_barrier(jnp.max(scores, axis=1, keepdims=True))
            expo = jnp.exp(scores - peak)
            totals = lax.optimization_barrier(jnp.sum(expo, axis=1))
            numerators = jnp.dot(expo.astype(jnp.bfloat16).astype(jnp.float32), head_values.astype(jnp.float32), preferred_element_type=jnp.float32)
            columns.append((numerators / totals[:, None]).astype(jnp.bfloat16))
    attention = jnp.concatenate(columns, axis=1)
    return jnp.dot(attention.astype(jnp.float32), out_proj.astype(jnp.float32), preferred_element_type=jnp.float32).astype(jnp.bfloat16)
```

```python
import functools

import jax
import jax.numpy as jnp
from jax import lax
from jax.experimental import pallas as pl
from jax.experimental.pallas import tpu as pltpu
from jax.sharding import PartitionSpec as P

BLOCK = 64
F32 = jnp.float32
BF16 = jnp.bfloat16
VMEM = pl.BlockSpec(memory_space=pltpu.VMEM)
SMEM = pl.BlockSpec(memory_space=pltpu.SMEM)


def mm(a, b):
    return lax.dot_general(
        a, b, (((1,), (0,)), ((), ())), precision=lax.Precision.HIGHEST, preferred_element_type=F32
    )


def mm_nt(a, b):
    return lax.dot_general(
        a, b, (((1,), (1,)), ((), ())), precision=lax.Precision.HIGHEST, preferred_element_type=F32
    )


def mm_fast(a, b):
    return lax.dot_general(a, b, (((1,), (0,)), ((), ())), preferred_element_type=F32)


def iotas(rows, cols):
    return (
        lax.broadcasted_iota(jnp.int32, (rows, cols), 0),
        lax.broadcasted_iota(jnp.int32, (rows, cols), 1),
    )


def eye(size):
    row, col = iotas(size, size)
    return jnp.where(row == col, 1.0, 0.0).astype(F32)


def chain(mats):
    mats = list(mats)
    while len(mats) > 1:
        mats = [
            mm(mats[i], mats[i + 1]) if i + 1 < len(mats) else mats[i]
            for i in range(0, len(mats), 2)
        ]
    return mats[0]


def call(kernel, outs, flops, **kw):
    single = not isinstance(outs, (tuple, list))
    many = (outs,) if single else tuple(outs)
    return pl.pallas_call(
        kernel,
        out_shape=outs if single else list(many),
        cost_estimate=pl.CostEstimate(flops=flops, bytes_accessed=1 << 20, transcendentals=0),
        **kw,
    )


def spans_kernel(raw_ref, total_ref, unit_ref, u_ref, parts_ref):
    raw = raw_ref[...].astype(F32)
    rows, width = raw.shape
    unit = raw * lax.rsqrt(jnp.sum(raw * raw, axis=-1, keepdims=True) + 1e-06)
    unit_ref[...] = unit
    turned = unit.T
    pair = 2 * BLOCK
    row, col = iotas(pair, pair)
    ident = eye(width)
    blocks = []
    for p in range(rows // pair):
        v = unit[p * pair : (p + 1) * pair]
        gram = mm_nt(v, v) * 2.0
        size = 1
        inv = jnp.where(row == col, 1.0, 0.0)
        while size < BLOCK:
            corner = (row // (2 * size) == col // (2 * size)) & (row // size < col // size)
            c = jnp.where(corner, gram, 0.0)
            if size == 1:
                inv = inv - c
            else:
                inv = inv - mm(inv, mm(c, inv))
            size *= 2
        u = mm(inv, v) * 2.0
        u_ref[p * pair : (p + 1) * pair, :] = u
        for b in range(2):
            lo = p * pair + b * BLOCK
            q = ident - mm(turned[:, lo : lo + BLOCK], u[b * BLOCK : (b + 1) * BLOCK])
            parts_ref[2 * p + b] = q
            blocks.append(q)
    total_ref[...] = chain(blocks)


def carry_kernel(half, keys_ref, unit_ref, u_ref, parts_ref, queries_ref, carried_ref, mixed_q_ref):
    keys = keys_ref[...].astype(F32)
    rows, width = keys.shape
    row, col = iotas(BLOCK, BLOCK)
    suffix = None
    for b in reversed(range(rows // BLOCK)):
        sl = slice(b * BLOCK, (b + 1) * BLOCK)
        k = keys[sl]
        inner = jnp.where(col > row, mm_nt(k, unit_ref[sl, :]), 0.0)
        done = k - mm(inner, u_ref[sl, :])
        carried_ref[sl, :] = done if suffix is None else mm(done, suffix)
        q = parts_ref[b]
        suffix = q if suffix is None else mm(q, suffix)
    mixed_q_ref[...] = reorder(half, queries_ref[...]).astype(BF16)


def reorder(half, x):
    halves, half_rows = half
    count = x.shape[0]
    row, col = iotas(count, count)
    group = halves * half_rows
    dest, rest = row // group, row % group
    source = (rest // half_rows) * (count // halves) + dest * half_rows + rest % half_rows
    return mm_fast(jnp.where(col == source, 1.0, 0.0).astype(BF16), x)


def sorted_slots(me, refs):
    vals = [r[...] for r in refs]
    slots = []
    for p in range(len(vals)):
        k = jnp.bitwise_xor(me, p)
        out = vals[0]
        for j in range(1, len(vals)):
            out = jnp.where(k == j, vals[j], out)
        slots.append(out)
    return slots


def digit(axis, stride, radix):
    return (lax.axis_index(axis) // stride) % radix


def total_kernel(stride, radix, *refs):
    *ins, out_ref = refs
    out_ref[...] = chain(sorted_slots(digit("seq", stride, radix), ins))


def later(me, slots):
    ident = eye(slots[0].shape[0])
    return [jnp.where(p > me, slots[p], ident) for p in range(1, len(slots))]


def shift_kernel(stride, radix, *refs):
    *ins, keys_ref, out_ref = refs
    me = digit("seq", stride, radix)
    out_ref[...] = mm(keys_ref[...], chain(later(me, sorted_slots(me, ins))))


def split3(x):
    hi = x.astype(BF16)
    rest = x - hi.astype(F32)
    mid = rest.astype(BF16)
    return hi, mid, (rest - mid.astype(F32)).astype(BF16)


def attend_kernel(stride, radix, heads, *refs):
    *ins, keys_ref, queries_ref, values_ref, out_ref = refs
    me = digit("seq", stride, radix)
    mats = later(me, sorted_slots(me, ins))
    width = keys_ref.shape[1]
    keys = mm(keys_ref[...], mats[0])
    rest = chain(mats[1:]) if len(mats) > 1 else None
    count = queries_ref.shape[0]
    dests, each = out_ref.shape[0], out_ref.shape[1]
    scale = 1.0 / (float(width) ** 0.5)
    lane = lax.broadcasted_iota(jnp.int32, (count, width), 1)
    stats = jnp.zeros((count, width), F32)
    for h in range(heads):
        q = queries_ref[:, h * width : (h + 1) * width].astype(F32)
        if rest is not None:
            q = mm_nt(q, rest)
        scores = mm_nt(q, keys) * scale
        peak = jnp.max(scores, axis=1, keepdims=True)
        expo = jnp.exp(scores - peak)
        total = jnp.sum(expo, axis=1, keepdims=True)
        numer = mm_fast(expo.astype(BF16), values_ref[...]) / total
        out_ref[:, :, h * width : (h + 1) * width] = numer.astype(BF16).reshape(dests, each, width)
        for i, part in enumerate(split3(peak) + split3(total)):
            stats = jnp.where(lane == h * 6 + i, part.astype(F32), stats)
    out_ref[:, :, heads * width :] = stats.astype(BF16).reshape(dests, each, width)


def merge(heads, width, got):
    stats = got[:, :, heads * width :].astype(F32)
    outs = []
    for h in range(heads):
        parts = [stats[:, :, h * 6 + i : h * 6 + i + 1] for i in range(6)]
        peak = parts[0] + parts[1] + parts[2]
        total = parts[3] + parts[4] + parts[5]
        weight = total * jnp.exp(peak - jnp.max(peak, axis=0, keepdims=True))
        weight = weight / jnp.sum(weight, axis=0, keepdims=True)
        numer = got[:, :, h * width : (h + 1) * width].astype(F32)
        outs.append(jnp.sum(weight * numer, axis=0))
    return outs


def merge_kernel(heads, halves, got_ref, out_ref):
    width = got_ref.shape[2] // (heads + 1)
    merged = merge(heads, width, got_ref[...])
    dests = out_ref.shape[0] // halves
    part = merged[0].shape[0] // halves
    stacked = jnp.concatenate(merged, axis=0).astype(BF16)
    rows = stacked.shape[0]
    row, col = iotas(rows, rows)
    p, h, j = row // (heads * part), (row // part) % heads, row % part
    pick = jnp.where(col == h * (halves * part) + p * part + j, 1.0, 0.0).astype(BF16)
    placed = mm_fast(pick, stacked).astype(BF16)
    each = heads * part
    for p in range(halves):
        piece = placed[p * each : (p + 1) * each]
        for s in range(dests):
            out_ref[s * halves + p] = piece


def project_kernel(heads, halves, got_ref, *refs):
    *w_refs, out_ref = refs
    me = lax.axis_index("head")
    sources, each, width = got_ref.shape
    part = each // heads
    rows = sources * each
    got = got_ref[...].reshape(rows, width)
    count = (sources // halves) * part
    row, col = iotas(rows, rows)
    g, h, s, j = row // (heads * count), (row // count) % heads, (row % count) // part, row % part
    pick = jnp.where(col == ((s * halves + g) * heads + h) * part + j, 1.0, 0.0).astype(BF16)
    placed = mm_fast(pick, got).astype(BF16)
    acc = jnp.zeros(out_ref.shape, F32)
    for k in range(halves):
        for h in range(heads):
            w = w_refs[0][h * width : (h + 1) * width, :]
            o = w_refs[1][h * width : (h + 1) * width, :] if halves > 1 else w
            w = jnp.where(me == k, w, o)
            lo = (k * heads + h) * count
            acc = acc + mm_fast(placed[lo : lo + count], w)
    out_ref[...] = acc.astype(BF16)


def radices(size):
    found = []
    while size % 4 == 0:
        found.append(4)
        size //= 4
    while size % 2 == 0:
        found.append(2)
        size //= 2
    assert size == 1
    return found


def exchange(x, devices, stride, radix):
    got = [x]
    for k in range(1, radix):
        pairs = []
        for i in range(devices):
            d = (i // stride) % radix
            pairs.append((i, i + ((d ^ k) - d) * stride))
        got.append(lax.ppermute(x, "seq", pairs))
    return got


def on_device(shards, halves, queries, keys, values, householder, out_proj):
    ctx_rows, width = keys.shape
    count = queries.shape[0]
    heads = queries.shape[1] // width
    each = count // shards
    direct = halves == 2 and each % halves == 0
    parts = (halves, each // halves) if direct else (1, each)
    square = jax.ShapeDtypeStruct((width, width), F32)
    tall = jax.ShapeDtypeStruct((ctx_rows, width), F32)
    blocks = ctx_rows // BLOCK
    if direct:
        other_w = lax.ppermute(out_proj, "head", [(0, 1), (1, 0)])
    total, unit, u, mats = call(
        spans_kernel,
        [square, tall, tall, jax.ShapeDtypeStruct((blocks, width, width), F32)],
        1 << 30,
    )(householder)
    rounds = []
    stride = 1
    for radix in radices(shards):
        rounds.append((stride, radix))
        stride *= radix
    carried = mixed_q = None
    for i, (stride, radix) in enumerate(rounds):
        got = exchange(total, shards, stride, radix)
        if i == 0:
            carried, mixed_q = call(
                functools.partial(carry_kernel, parts),
                [tall, jax.ShapeDtypeStruct(queries.shape, BF16)],
                1 << 31,
            )(keys, unit, u, mats, queries)
        if i + 1 < len(rounds):
            total = call(functools.partial(total_kernel, stride, radix), square, 1 << 28)(*got)
            carried = call(functools.partial(shift_kernel, stride, radix), tall, 1 << 30)(
                *got, carried
            )
    packed = call(
        functools.partial(attend_kernel, stride, radix, heads),
        jax.ShapeDtypeStruct((shards, each, (heads + 1) * width), BF16),
        1 << 31,
    )(*got, carried, mixed_q, values)
    packed = lax.all_to_all(packed, "seq", split_axis=0, concat_axis=0, tiled=True)
    if direct:
        spread = call(
            functools.partial(merge_kernel, heads, halves),
            jax.ShapeDtypeStruct((shards * halves, heads * each // halves, width), BF16),
            1 << 26,
        )(packed)
        spread = lax.all_to_all(spread, ("seq", "head"), split_axis=0, concat_axis=0, tiled=True)
        return call(
            functools.partial(project_kernel, heads, halves),
            jax.ShapeDtypeStruct((count // halves, out_proj.shape[1]), BF16),
            1 << 28,
        )(spread, out_proj, other_w)
    rows = jnp.concatenate(merge(heads, width, packed), axis=1).astype(BF16)
    attention = lax.all_gather(rows, "seq", axis=0, tiled=True)
    mixed = jnp.dot(attention, out_proj, preferred_element_type=F32).astype(BF16)
    return lax.psum_scatter(mixed, "head", scatter_dimension=0, tiled=True)


def solution(mesh):
    placed = (
        P(None, "head"),
        P("seq", "head"),
        P("seq", "head"),
        P("seq", "head"),
        P("head", "seq"),
    )
    body = functools.partial(on_device, mesh.shape["seq"], mesh.shape["head"])
    return jax.shard_map(
        body, mesh=mesh, in_specs=placed, out_specs=P("head", "seq"), check_vma=False
    )
```

```python
import functools

import jax
import jax.numpy as jnp
from jax import lax
from jax.experimental import pallas as pl
from jax.experimental.pallas import tpu as pltpu
from jax.sharding import PartitionSpec as P

BLOCK = 64
LIMIT = 16 << 20
F32 = jnp.float32
BF16 = jnp.bfloat16
VMEM = pl.BlockSpec(memory_space=pltpu.VMEM)
SMEM = pl.BlockSpec(memory_space=pltpu.SMEM)


def mm(a, b):
    return lax.dot_general(
        a, b, (((1,), (0,)), ((), ())), precision=lax.Precision.HIGHEST, preferred_element_type=F32
    )


def mm_nt(a, b):
    return lax.dot_general(
        a, b, (((1,), (1,)), ((), ())), precision=lax.Precision.HIGHEST, preferred_element_type=F32
    )


def mm_fast(a, b):
    return lax.dot_general(a, b, (((1,), (0,)), ((), ())), preferred_element_type=F32)


def iotas(rows, cols):
    return (
        lax.broadcasted_iota(jnp.int32, (rows, cols), 0),
        lax.broadcasted_iota(jnp.int32, (rows, cols), 1),
    )


def eye(size):
    row, col = iotas(size, size)
    return jnp.where(row == col, 1.0, 0.0).astype(F32)


def chain(mats):
    mats = list(mats)
    while len(mats) > 1:
        mats = [
            mm(mats[i], mats[i + 1]) if i + 1 < len(mats) else mats[i]
            for i in range(0, len(mats), 2)
        ]
    return mats[0]


def call(kernel, outs, flops, **kw):
    single = not isinstance(outs, (tuple, list))
    many = (outs,) if single else tuple(outs)
    return pl.pallas_call(
        kernel,
        out_shape=outs if single else list(many),
        cost_estimate=pl.CostEstimate(flops=flops, bytes_accessed=1 << 20, transcendentals=0),
        compiler_params=pltpu.CompilerParams(vmem_limit_bytes=LIMIT),
        **kw,
    )


def spans_kernel(raw_ref, total_ref, unit_ref, u_ref, parts_ref):
    raw = raw_ref[...].astype(F32)
    rows, width = raw.shape
    unit = raw * lax.rsqrt(jnp.sum(raw * raw, axis=-1, keepdims=True) + 1e-06)
    unit_ref[...] = unit
    turned = unit.T
    pair = 2 * BLOCK
    row, col = iotas(pair, pair)
    ident = eye(width)
    blocks = []
    for p in range(rows // pair):
        v = unit[p * pair : (p + 1) * pair]
        gram = mm_nt(v, v) * 2.0
        size = 1
        inv = jnp.where(row == col, 1.0, 0.0)
        while size < BLOCK:
            corner = (row // (2 * size) == col // (2 * size)) & (row // size < col // size)
            c = jnp.where(corner, gram, 0.0)
            if size == 1:
                inv = inv - c
            else:
                inv = inv - mm(inv, mm(c, inv))
            size *= 2
        u = mm(inv, v) * 2.0
        u_ref[p * pair : (p + 1) * pair, :] = u
        for b in range(2):
            lo = p * pair + b * BLOCK
            q = ident - mm(turned[:, lo : lo + BLOCK], u[b * BLOCK : (b + 1) * BLOCK])
            parts_ref[2 * p + b] = q
            blocks.append(q)
    total_ref[...] = chain(blocks)


def carry_kernel(half, keys_ref, unit_ref, u_ref, parts_ref, queries_ref, carried_ref, mixed_q_ref):
    keys = keys_ref[...].astype(F32)
    rows, width = keys.shape
    row, col = iotas(BLOCK, BLOCK)
    suffix = None
    for b in reversed(range(rows // BLOCK)):
        sl = slice(b * BLOCK, (b + 1) * BLOCK)
        k = keys[sl]
        inner = jnp.where(col > row, mm_nt(k, unit_ref[sl, :]), 0.0)
        done = k - mm(inner, u_ref[sl, :])
        carried_ref[sl, :] = done if suffix is None else mm(done, suffix)
        q = parts_ref[b]
        suffix = q if suffix is None else mm(q, suffix)
    mixed_q_ref[...] = reorder(half, queries_ref[...]).astype(BF16)


def reorder(half, x):
    halves, half_rows = half
    count = x.shape[0]
    row, col = iotas(count, count)
    group = halves * half_rows
    dest, rest = row // group, row % group
    source = (rest // half_rows) * (count // halves) + dest * half_rows + rest % half_rows
    return mm_fast(jnp.where(col == source, 1.0, 0.0).astype(BF16), x)


def sorted_slots(me, refs):
    vals = [r[...] for r in refs]
    slots = []
    for p in range(len(vals)):
        k = jnp.bitwise_xor(me, p)
        out = vals[0]
        for j in range(1, len(vals)):
            out = jnp.where(k == j, vals[j], out)
        slots.append(out)
    return slots


def digit(axis, stride, radix):
    return (lax.axis_index(axis) // stride) % radix


def total_kernel(stride, radix, *refs):
    *ins, out_ref = refs
    out_ref[...] = chain(sorted_slots(digit("seq", stride, radix), ins))


def later(me, slots):
    ident = eye(slots[0].shape[0])
    return [jnp.where(p > me, slots[p], ident) for p in range(1, len(slots))]


def shift_kernel(stride, radix, *refs):
    *ins, keys_ref, out_ref = refs
    me = digit("seq", stride, radix)
    out_ref[...] = mm(keys_ref[...], chain(later(me, sorted_slots(me, ins))))


def split3(x):
    hi = x.astype(BF16)
    rest = x - hi.astype(F32)
    mid = rest.astype(BF16)
    return hi, mid, (rest - mid.astype(F32)).astype(BF16)


def attend_kernel(stride, radix, heads, *refs):
    *ins, keys_ref, queries_ref, values_ref, out_ref = refs
    me = digit("seq", stride, radix)
    mats = later(me, sorted_slots(me, ins))
    width = keys_ref.shape[1]
    keys = mm(keys_ref[...], mats[0])
    rest = chain(mats[1:]) if len(mats) > 1 else None
    count = queries_ref.shape[0]
    dests, each = out_ref.shape[0], out_ref.shape[1]
    scale = 1.0 / (float(width) ** 0.5)
    lane = lax.broadcasted_iota(jnp.int32, (count, width), 1)
    stats = jnp.zeros((count, width), F32)
    for h in range(heads):
        q = queries_ref[:, h * width : (h + 1) * width].astype(F32)
        if rest is not None:
            q = mm_nt(q, rest)
        scores = mm_nt(q, keys) * scale
        peak = jnp.max(scores, axis=1, keepdims=True)
        expo = jnp.exp(scores - peak)
        total = jnp.sum(expo, axis=1, keepdims=True)
        numer = mm_fast(expo.astype(BF16), values_ref[...]) / total
        out_ref[:, :, h * width : (h + 1) * width] = numer.astype(BF16).reshape(dests, each, width)
        for i, part in enumerate(split3(peak) + split3(total)):
            stats = jnp.where(lane == h * 6 + i, part.astype(F32), stats)
    out_ref[:, :, heads * width :] = stats.astype(BF16).reshape(dests, each, width)


def merge(heads, width, got):
    stats = got[:, :, heads * width :].astype(F32)
    outs = []
    for h in range(heads):
        parts = [stats[:, :, h * 6 + i : h * 6 + i + 1] for i in range(6)]
        peak = parts[0] + parts[1] + parts[2]
        total = parts[3] + parts[4] + parts[5]
        weight = total * jnp.exp(peak - jnp.max(peak, axis=0, keepdims=True))
        weight = weight / jnp.sum(weight, axis=0, keepdims=True)
        numer = got[:, :, h * width : (h + 1) * width].astype(F32)
        outs.append(jnp.sum(weight * numer, axis=0))
    return outs


def merge_kernel(heads, halves, got_ref, out_ref):
    width = got_ref.shape[2] // (heads + 1)
    merged = merge(heads, width, got_ref[...])
    dests = out_ref.shape[0] // halves
    part = merged[0].shape[0] // halves
    stacked = jnp.concatenate(merged, axis=0).astype(BF16)
    rows = stacked.shape[0]
    row, col = iotas(rows, rows)
    p, h, j = row // (heads * part), (row // part) % heads, row % part
    pick = jnp.where(col == h * (halves * part) + p * part + j, 1.0, 0.0).astype(BF16)
    placed = mm_fast(pick, stacked).astype(BF16)
    each = heads * part
    for p in range(halves):
        piece = placed[p * each : (p + 1) * each]
        for s in range(dests):
            out_ref[s * halves + p] = piece


def project_kernel(heads, halves, got_ref, *refs):
    *w_refs, out_ref = refs
    me = lax.axis_index("head")
    sources, each, width = got_ref.shape
    part = each // heads
    rows = sources * each
    got = got_ref[...].reshape(rows, width)
    count = (sources // halves) * part
    row, col = iotas(rows, rows)
    g, h, s, j = row // (heads * count), (row // count) % heads, (row % count) // part, row % part
    pick = jnp.where(col == ((s * halves + g) * heads + h) * part + j, 1.0, 0.0).astype(BF16)
    placed = mm_fast(pick, got).astype(BF16)
    acc = jnp.zeros(out_ref.shape, F32)
    for k in range(halves):
        for h in range(heads):
            w = w_refs[0][h * width : (h + 1) * width, :]
            o = w_refs[1][h * width : (h + 1) * width, :] if halves > 1 else w
            w = jnp.where(me == k, w, o)
            lo = (k * heads + h) * count
            acc = acc + mm_fast(placed[lo : lo + count], w)
    out_ref[...] = acc.astype(BF16)


def radices(size):
    found = []
    while size % 4 == 0:
        found.append(4)
        size //= 4
    while size % 2 == 0:
        found.append(2)
        size //= 2
    assert size == 1
    return found


def exchange(x, devices, stride, radix):
    got = [x]
    for k in range(1, radix):
        pairs = []
        for i in range(devices):
            d = (i // stride) % radix
            pairs.append((i, i + ((d ^ k) - d) * stride))
        got.append(lax.ppermute(x, "seq", pairs))
    return got


def on_device(shards, halves, queries, keys, values, householder, out_proj):
    ctx_rows, width = keys.shape
    count = queries.shape[0]
    heads = queries.shape[1] // width
    each = count // shards
    direct = halves == 2 and each % halves == 0
    parts = (halves, each // halves) if direct else (1, each)
    square = jax.ShapeDtypeStruct((width, width), F32)
    tall = jax.ShapeDtypeStruct((ctx_rows, width), F32)
    blocks = ctx_rows // BLOCK
    if direct:
        other_w = lax.ppermute(out_proj, "head", [(0, 1), (1, 0)])
    total, unit, u, mats = call(
        spans_kernel,
        [square, tall, tall, jax.ShapeDtypeStruct((blocks, width, width), F32)],
        1 << 30,
    )(householder)
    rounds = []
    stride = 1
    for radix in radices(shards):
        rounds.append((stride, radix))
        stride *= radix
    carried = mixed_q = None
    for i, (stride, radix) in enumerate(rounds):
        got = exchange(total, shards, stride, radix)
        if i == 0:
            carried, mixed_q = call(
                functools.partial(carry_kernel, parts),
                [tall, jax.ShapeDtypeStruct(queries.shape, BF16)],
                1 << 31,
            )(keys, unit, u, mats, queries)
        if i + 1 < len(rounds):
            total = call(functools.partial(total_kernel, stride, radix), square, 1 << 28)(*got)
            carried = call(functools.partial(shift_kernel, stride, radix), tall, 1 << 30)(
                *got, carried
            )
    packed = call(
        functools.partial(attend_kernel, stride, radix, heads),
        jax.ShapeDtypeStruct((shards, each, (heads + 1) * width), BF16),
        1 << 31,
    )(*got, carried, mixed_q, values)
    packed = lax.all_to_all(packed, "seq", split_axis=0, concat_axis=0, tiled=True)
    if direct:
        spread = call(
            functools.partial(merge_kernel, heads, halves),
            jax.ShapeDtypeStruct((shards * halves, heads * each // halves, width), BF16),
            1 << 26,
        )(packed)
        spread = lax.all_to_all(spread, ("seq", "head"), split_axis=0, concat_axis=0, tiled=True)
        return call(
            functools.partial(project_kernel, heads, halves),
            jax.ShapeDtypeStruct((count // halves, out_proj.shape[1]), BF16),
            1 << 28,
        )(spread, out_proj, other_w)
    rows = jnp.concatenate(merge(heads, width, packed), axis=1).astype(BF16)
    attention = lax.all_gather(rows, "seq", axis=0, tiled=True)
    mixed = jnp.dot(attention, out_proj, preferred_element_type=F32).astype(BF16)
    return lax.psum_scatter(mixed, "head", scatter_dimension=0, tiled=True)


def solution(mesh):
    placed = (
        P(None, "head"),
        P("seq", "head"),
        P("seq", "head"),
        P("seq", "head"),
        P("head", "seq"),
    )
    body = functools.partial(on_device, mesh.shape["seq"], mesh.shape["head"])
    return jax.shard_map(
        body, mesh=mesh, in_specs=placed, out_specs=P("head", "seq"), check_vma=False
    )
```

```python
import functools

import jax
import jax.numpy as jnp
from jax import lax
from jax.experimental import pallas as pl
from jax.experimental.pallas import tpu as pltpu
from jax.sharding import PartitionSpec as P

BLOCK = 64
SMALL = 16
LIMIT = 16 << 20
F32 = jnp.float32
BF16 = jnp.bfloat16
VMEM = pl.BlockSpec(memory_space=pltpu.VMEM)
SMEM = pl.BlockSpec(memory_space=pltpu.SMEM)


def halves_of(x):
    hi = x.astype(BF16)
    return hi, (x - hi.astype(F32)).astype(BF16)


def wide(x):
    return jnp.concatenate(halves_of(x), axis=1)


def deep(x):
    hi, lo = halves_of(x)
    both = jnp.concatenate([hi, lo], axis=1)
    return jnp.concatenate([both, both], axis=0)


def deep_nt(x):
    hi, lo = halves_of(x)
    return jnp.concatenate(
        [jnp.concatenate([hi, hi], axis=1), jnp.concatenate([lo, lo], axis=1)], axis=0
    )


def fold(x):
    half = x.shape[1] // 2
    return x[:, :half] + x[:, half:]


def mm(a, b):
    return fold(
        lax.dot_general(wide(a), deep(b), (((1,), (0,)), ((), ())), preferred_element_type=F32)
    )


def mm_nt(a, b):
    return fold(
        lax.dot_general(wide(a), deep_nt(b), (((1,), (1,)), ((), ())), preferred_element_type=F32)
    )


def mm_fast(a, b):
    return lax.dot_general(a, b, (((1,), (0,)), ((), ())), preferred_element_type=F32)


def iotas(rows, cols):
    return (
        lax.broadcasted_iota(jnp.int32, (rows, cols), 0),
        lax.broadcasted_iota(jnp.int32, (rows, cols), 1),
    )


def eye(size):
    row, col = iotas(size, size)
    return jnp.where(row == col, 1.0, 0.0).astype(F32)


def chain(mats):
    mats = list(mats)
    while len(mats) > 1:
        mats = [
            mm(mats[i], mats[i + 1]) if i + 1 < len(mats) else mats[i]
            for i in range(0, len(mats), 2)
        ]
    return mats[0]


def call(kernel, outs, flops, **kw):
    single = not isinstance(outs, (tuple, list))
    many = (outs,) if single else tuple(outs)
    return pl.pallas_call(
        kernel,
        out_shape=outs if single else list(many),
        cost_estimate=pl.CostEstimate(flops=flops, bytes_accessed=1 << 20, transcendentals=0),
        compiler_params=pltpu.CompilerParams(vmem_limit_bytes=LIMIT),
        **kw,
    )


def small_inverses(grams):
    size = grams[0].shape[0]
    count = size // SMALL
    row, lane = iotas(SMALL, size)
    first = lane // SMALL * SMALL
    packs, invs = [], []
    for gram in grams:
        packed = jnp.zeros((SMALL, size), F32)
        for b in range(count):
            packed = jnp.where(lane // SMALL == b, gram[b * SMALL : (b + 1) * SMALL], packed)
        packs.append(jnp.where(row < lane % SMALL, packed, 0.0))
        invs.append(jnp.where(row == lane % SMALL, 1.0, 0.0))
    for k in reversed(range(1, SMALL)):
        columns = [jnp.take_along_axis(packed, first + k, axis=1) for packed in packs]
        invs = [inv - column * inv[k : k + 1] for inv, column in zip(invs, columns)]
    row, col = iotas(size, size)
    same = row // SMALL == col // SMALL
    return [jnp.where(same, jnp.concatenate([inv] * count, axis=0), 0.0) for inv in invs]


def spans_kernel(raw_ref, total_ref, unit_ref, u_ref, parts_ref):
    raw = raw_ref[...].astype(F32)
    rows, width = raw.shape
    unit = raw * lax.rsqrt(jnp.sum(raw * raw, axis=-1, keepdims=True) + 1e-06)
    unit_ref[...] = unit
    turned = unit.T
    pair = 2 * BLOCK
    pairs = range(rows // pair)
    row, col = iotas(pair, pair)
    ident = eye(width)
    vs = [unit[p * pair : (p + 1) * pair] for p in pairs]
    grams = [mm_nt(v, v) * 2.0 for v in vs]
    size = SMALL
    invs = small_inverses(grams)
    while size < BLOCK:
        corner = (row // (2 * size) == col // (2 * size)) & (row // size < col // size)
        steps = [mm(jnp.where(corner, g, 0.0), z) for g, z in zip(grams, invs)]
        invs = [z - mm(z, t) for z, t in zip(invs, steps)]
        size *= 2
    us = [mm(z, v) * 2.0 for z, v in zip(invs, vs)]
    blocks = []
    for p in pairs:
        u_ref[p * pair : (p + 1) * pair, :] = us[p]
        for b in range(2):
            lo = p * pair + b * BLOCK
            blocks.append(ident - mm(turned[:, lo : lo + BLOCK], us[p][b * BLOCK : (b + 1) * BLOCK]))
    for b, q in enumerate(blocks):
        parts_ref[b] = q
    total_ref[...] = chain(blocks)


def carry_kernel(half, keys_ref, unit_ref, u_ref, parts_ref, queries_ref, carried_ref, mixed_q_ref):
    keys = keys_ref[...].astype(F32)
    rows, width = keys.shape
    row, col = iotas(BLOCK, BLOCK)
    suffix = None
    for b in reversed(range(rows // BLOCK)):
        sl = slice(b * BLOCK, (b + 1) * BLOCK)
        k = keys[sl]
        inner = jnp.where(col > row, mm_nt(k, unit_ref[sl, :]), 0.0)
        done = k - mm(inner, u_ref[sl, :])
        carried_ref[sl, :] = done if suffix is None else mm(done, suffix)
        q = parts_ref[b]
        suffix = q if suffix is None else mm(q, suffix)
    mixed_q_ref[...] = reorder(half, queries_ref[...]).astype(BF16)


def reorder(half, x):
    halves, half_rows = half
    count = x.shape[0]
    row, col = iotas(count, count)
    group = halves * half_rows
    dest, rest = row // group, row % group
    source = (rest // half_rows) * (count // halves) + dest * half_rows + rest % half_rows
    return mm_fast(jnp.where(col == source, 1.0, 0.0).astype(BF16), x)


def sorted_slots(me, refs):
    vals = [r[...] for r in refs]
    slots = []
    for p in range(len(vals)):
        k = jnp.bitwise_xor(me, p)
        out = vals[0]
        for j in range(1, len(vals)):
            out = jnp.where(k == j, vals[j], out)
        slots.append(out)
    return slots


def digit(axis, stride, radix):
    return (lax.axis_index(axis) // stride) % radix


def total_kernel(stride, radix, *refs):
    *ins, out_ref = refs
    out_ref[...] = chain(sorted_slots(digit("seq", stride, radix), ins))


def later(me, slots):
    ident = eye(slots[0].shape[0])
    return [jnp.where(p > me, slots[p], ident) for p in range(1, len(slots))]


def shift_kernel(stride, radix, *refs):
    *ins, keys_ref, out_ref = refs
    me = digit("seq", stride, radix)
    out_ref[...] = mm(keys_ref[...], chain(later(me, sorted_slots(me, ins))))


def split3(x):
    hi = x.astype(BF16)
    rest = x - hi.astype(F32)
    mid = rest.astype(BF16)
    return hi, mid, (rest - mid.astype(F32)).astype(BF16)


def attend_kernel(stride, radix, heads, *refs):
    *ins, keys_ref, queries_ref, values_ref, out_ref = refs
    me = digit("seq", stride, radix)
    mats = later(me, sorted_slots(me, ins))
    width = keys_ref.shape[1]
    keys = mm(keys_ref[...], mats[0])
    rest = chain(mats[1:]) if len(mats) > 1 else None
    count = queries_ref.shape[0]
    dests, each = out_ref.shape[0], out_ref.shape[1]
    scale = 1.0 / (float(width) ** 0.5)
    lane = lax.broadcasted_iota(jnp.int32, (count, width), 1)
    stats = jnp.zeros((count, width), F32)
    for h in range(heads):
        q = queries_ref[:, h * width : (h + 1) * width].astype(F32)
        if rest is not None:
            q = mm_nt(q, rest)
        scores = mm_nt(q, keys) * scale
        peak = jnp.max(scores, axis=1, keepdims=True)
        expo = jnp.exp(scores - peak)
        total = jnp.sum(expo, axis=1, keepdims=True)
        numer = mm_fast(expo.astype(BF16), values_ref[...]) / total
        out_ref[:, :, h * width : (h + 1) * width] = numer.astype(BF16).reshape(dests, each, width)
        for i, part in enumerate(split3(peak) + split3(total)):
            stats = jnp.where(lane == h * 6 + i, part.astype(F32), stats)
    out_ref[:, :, heads * width :] = stats.astype(BF16).reshape(dests, each, width)


def merge(heads, width, got):
    stats = got[:, :, heads * width :].astype(F32)
    outs = []
    for h in range(heads):
        parts = [stats[:, :, h * 6 + i : h * 6 + i + 1] for i in range(6)]
        peak = parts[0] + parts[1] + parts[2]
        total = parts[3] + parts[4] + parts[5]
        weight = total * jnp.exp(peak - jnp.max(peak, axis=0, keepdims=True))
        weight = weight / jnp.sum(weight, axis=0, keepdims=True)
        numer = got[:, :, h * width : (h + 1) * width].astype(F32)
        outs.append(jnp.sum(weight * numer, axis=0))
    return outs


def merge_kernel(heads, halves, got_ref, out_ref):
    width = got_ref.shape[2] // (heads + 1)
    merged = merge(heads, width, got_ref[...])
    dests = out_ref.shape[0] // halves
    part = merged[0].shape[0] // halves
    stacked = jnp.concatenate(merged, axis=0).astype(BF16)
    rows = stacked.shape[0]
    row, col = iotas(rows, rows)
    p, h, j = row // (heads * part), (row // part) % heads, row % part
    pick = jnp.where(col == h * (halves * part) + p * part + j, 1.0, 0.0).astype(BF16)
    placed = mm_fast(pick, stacked).astype(BF16)
    each = heads * part
    for p in range(halves):
        piece = placed[p * each : (p + 1) * each]
        for s in range(dests):
            out_ref[s * halves + p] = piece


def project_kernel(heads, halves, got_ref, *refs):
    *w_refs, out_ref = refs
    me = lax.axis_index("head")
    sources, each, width = got_ref.shape
    part = each // heads
    rows = sources * each
    got = got_ref[...].reshape(rows, width)
    count = (sources // halves) * part
    row, col = iotas(rows, rows)
    g, h, s, j = row // (heads * count), (row // count) % heads, (row % count) // part, row % part
    pick = jnp.where(col == ((s * halves + g) * heads + h) * part + j, 1.0, 0.0).astype(BF16)
    placed = mm_fast(pick, got).astype(BF16)
    acc = jnp.zeros(out_ref.shape, F32)
    for k in range(halves):
        for h in range(heads):
            w = w_refs[0][h * width : (h + 1) * width, :]
            o = w_refs[1][h * width : (h + 1) * width, :] if halves > 1 else w
            w = jnp.where(me == k, w, o)
            lo = (k * heads + h) * count
            acc = acc + mm_fast(placed[lo : lo + count], w)
    out_ref[...] = acc.astype(BF16)


def radices(size):
    found = []
    while size % 4 == 0:
        found.append(4)
        size //= 4
    while size % 2 == 0:
        found.append(2)
        size //= 2
    assert size == 1
    return found


def exchange(x, devices, stride, radix):
    got = [x]
    for k in range(1, radix):
        pairs = []
        for i in range(devices):
            d = (i // stride) % radix
            pairs.append((i, i + ((d ^ k) - d) * stride))
        got.append(lax.ppermute(x, "seq", pairs))
    return got


def on_device(shards, halves, queries, keys, values, householder, out_proj):
    ctx_rows, width = keys.shape
    count = queries.shape[0]
    heads = queries.shape[1] // width
    each = count // shards
    direct = halves == 2 and each % halves == 0
    parts = (halves, each // halves) if direct else (1, each)
    square = jax.ShapeDtypeStruct((width, width), F32)
    tall = jax.ShapeDtypeStruct((ctx_rows, width), F32)
    blocks = ctx_rows // BLOCK
    if direct:
        other_w = lax.ppermute(out_proj, "head", [(0, 1), (1, 0)])
    total, unit, u, mats = call(
        spans_kernel,
        [square, tall, tall, jax.ShapeDtypeStruct((blocks, width, width), F32)],
        1 << 30,
    )(householder)
    rounds = []
    stride = 1
    for radix in radices(shards):
        rounds.append((stride, radix))
        stride *= radix
    carried = mixed_q = None
    for i, (stride, radix) in enumerate(rounds):
        got = exchange(total, shards, stride, radix)
        if i == 0:
            carried, mixed_q = call(
                functools.partial(carry_kernel, parts),
                [tall, jax.ShapeDtypeStruct(queries.shape, BF16)],
                1 << 31,
            )(keys, unit, u, mats, queries)
        if i + 1 < len(rounds):
            total = call(functools.partial(total_kernel, stride, radix), square, 1 << 28)(*got)
            carried = call(functools.partial(shift_kernel, stride, radix), tall, 1 << 30)(
                *got, carried
            )
    packed = call(
        functools.partial(attend_kernel, stride, radix, heads),
        jax.ShapeDtypeStruct((shards, each, (heads + 1) * width), BF16),
        1 << 31,
    )(*got, carried, mixed_q, values)
    packed = lax.all_to_all(packed, "seq", split_axis=0, concat_axis=0, tiled=True)
    if direct:
        spread = call(
            functools.partial(merge_kernel, heads, halves),
            jax.ShapeDtypeStruct((shards * halves, heads * each // halves, width), BF16),
            1 << 26,
        )(packed)
        spread = lax.all_to_all(spread, ("seq", "head"), split_axis=0, concat_axis=0, tiled=True)
        return call(
            functools.partial(project_kernel, heads, halves),
            jax.ShapeDtypeStruct((count // halves, out_proj.shape[1]), BF16),
            1 << 28,
        )(spread, out_proj, other_w)
    rows = jnp.concatenate(merge(heads, width, packed), axis=1).astype(BF16)
    attention = lax.all_gather(rows, "seq", axis=0, tiled=True)
    mixed = jnp.dot(attention, out_proj, preferred_element_type=F32).astype(BF16)
    return lax.psum_scatter(mixed, "head", scatter_dimension=0, tiled=True)


def solution(mesh):
    placed = (
        P(None, "head"),
        P("seq", "head"),
        P("seq", "head"),
        P("seq", "head"),
        P("head", "seq"),
    )
    body = functools.partial(on_device, mesh.shape["seq"], mesh.shape["head"])
    return jax.shard_map(
        body, mesh=mesh, in_specs=placed, out_specs=P("head", "seq"), check_vma=False
    )
```
